1024 devices in a mesh: dp: 64 (over y_hi, z, core), tensor: 16 (over x, y_lo).
Axes of the slice: x: 4, y: 8 (y_hi: 2, y_lo: 4; y = y_hi * 4 + y_lo), z: 16, core: 2. Of those that a mesh axis runs over, the one named last changes fastest.
Arguments:
- acts: bfloat16 [8192, 8192], P('dp', 'tensor'), may hold values from -6 to 6
- grad_out: bfloat16 [8192, 14336], P('dp', 'tensor'), may hold values from -6 to 6
- proj_t: bfloat16 [512, 8192], P(None, 'tensor'), may hold values from -6 to 6
- first_moment: float32 [512, 14336], P('dp', 'tensor'), may hold values from -0.15625 to 0.15625
- second_moment: float32 [512, 14336], P('dp', 'tensor'), may hold values from 1e-05 to 0.001
Outputs:
- adam_step: float32 [512, 14336], P('dp', 'tensor')
- new_proj_t: float32 [512, 8192], P('dp', 'tensor')
The draws below stay inside these ranges and needn't reach their ends.
All inputs are finite; a program needn't handle non-finite values.
Results may differ from the reference program's by a relative error of at most 0.023.
Values may be sent and summed in bfloat16 or wider, within the bound.
No kernel may reach another device: no remote copies, remote signals or barrier semaphores. Data moves between devices by JAX's collectives and lax.ppermute only.
A program may use at most 32 MiB of HBM per device.

```python
import math
import jax
import jax.numpy as jnp
from jax import lax

D = 8192
F = 14336
R = 512
TOKENS = 8192
N_TENSOR = 16


def block_levels(stream_key, dims, shards, least, high):
    loudness, own = 1.0, jax.random.fold_in(stream_key, 6)
    for position, parts in shards:
        draws = jnp.exp(jax.random.uniform(jax.random.fold_in(own, position), (parts,), jnp.float32, least / len(shards), high / len(shards)))
        loudness = loudness * jnp.repeat(draws, dims[position] // parts).reshape([-1 if axis == position else 1 for axis in range(len(dims))])
    return loudness


def bell_draw(key, shape, deviation, bound, pieces=(), held_as=jnp.bfloat16):
    entries = jax.random.normal(key, shape, jnp.float32) * deviation
    if len(pieces) > 0:
        entries = block_levels(key, shape, pieces, -0.22, 0.18) * entries
    return jnp.clip(entries, min=-bound, max=bound).astype(held_as)


def setup_inputs(seed: int = 0) -> dict:
    arg_keys = jax.random.split(jax.random.key(seed), 6)
    return {
        "acts": bell_draw(arg_keys[0], (TOKENS, D), 1.0, 6.0, ((0, 64), (1, 16))),
        "grad_out": bell_draw(arg_keys[1], (TOKENS, F), 1.0, 6.0, ((0, 64), (1, 16))),
        "proj_t": bell_draw(arg_keys[2], (R, D), 1.0, 6.0, ((1, 16),)),
        "first_moment": bell_draw(arg_keys[3], (R, F), 0.01, 0.15625, ((0, 64), (1, 16)), jnp.float32),
        "second_moment": jnp.clip(jnp.exp(math.log(0.001) - 4.6051703 * jax.random.uniform(arg_keys[4], (R, F), jnp.float32) ** block_levels(arg_keys[4], (R, F), ((0, 64), (1, 16)), -0.2, 0.2)), 9.999999747378752e-06, 0.001),
    }


def rounded_sum(terms):
    total = jnp.zeros(terms[0].shape, jnp.float32)
    for term in terms:
        low_term = lax.optimization_barrier(term.astype(jnp.bfloat16))
        total = total + low_term.astype(jnp.float32)
    return total

def reference(acts, grad_out, proj_t, first_moment, second_moment):
    inv_root = 1.0 / jnp.sqrt(jnp.float32(D))
    width_blk = D // N_TENSOR
    hidden_blk = F // N_TENSOR
    coord_terms = []
    for block in range(N_TENSOR):
        lo = block * width_blk
        part = lax.dot_general(acts[:, lo:lo + width_blk], proj_t[:, lo:lo + width_blk], (((1,), (1,)), ((), ())), preferred_element_type=jnp.float32)
        coord_terms.append(part * inv_root)
    coords = rounded_sum(coord_terms).astype(jnp.bfloat16)
    proj_grad = lax.dot_general(coords, grad_out, (((0,), (0,)), ((), ())), preferred_element_type=jnp.float32) / TOKENS
    moment_one = 0.9 * first_moment + 0.1 * proj_grad
    moment_two = 0.999 * second_moment + 0.001 * proj_grad * proj_grad
    adam_step = moment_one / (1.0 - 0.9 ** 10) / (jnp.sqrt(moment_two / (1.0 - 0.999 ** 10)) + 1e-08)
    low = proj_grad.astype(jnp.bfloat16)
    back_terms = []
    cross_terms = []
    for block in range(N_TENSOR):
        lo = block * hidden_blk
        low_blk = low[:, lo:lo + hidden_blk]
        back_terms.append(lax.dot_general(grad_out[:, lo:lo + hidden_blk], low_blk, (((1,), (1,)), ((), ())), preferred_element_type=jnp.float32))
        cross_terms.append(lax.dot_general(low_blk, low_blk, (((1,), (1,)), ((), ())), preferred_element_type=jnp.float32))
    back = rounded_sum(back_terms)
    cross = rounded_sum(cross_terms)
    back_low = back.astype(jnp.bfloat16)
    pull = lax.dot_general(back_low, acts, (((0,), (0,)), ((), ())), preferred_element_type=jnp.float32) / TOKENS
    proj_wide = proj_t.astype(jnp.float32)
    correction = jnp.dot(cross, proj_wide, precision=lax.Precision.HIGHEST)
    new_proj_t = proj_wide + jnp.sqrt(jnp.float32(D)) * pull - correction
    return (adam_step, new_proj_t)
```

```python
import math

import jax
import jax.numpy as jnp
from jax import lax
from jax.sharding import Mesh, PartitionSpec as P

D = 8192
TOKENS = 8192
DP = ("yh", "z3", "z2", "z1", "z0", "c")
SIZES = (2, 2, 2, 2, 2, 2)
TENSOR = ("x", "yl")
NEAR = ("c",)
FAR = tuple(a for a in DP if a not in NEAR)


def size(axes):
    return math.prod(SIZES[DP.index(a)] for a in axes)


def swap(pieces, axes):
    return lax.all_to_all(pieces, axes, split_axis=0, concat_axis=0, tiled=True)


def to_all(x, axes, count):
    return swap(jnp.broadcast_to(x, (count, *x.shape)), axes)


def total(pieces):
    return jnp.sum(pieces.astype(jnp.float32), axis=0)


def dot(left, right, dims):
    return lax.dot_general(left, right, (dims, ((), ())), preferred_element_type=jnp.float32)


def by_near(x):
    rows, cols = x.shape
    order = [DP.index(a) for a in NEAR + FAR]
    x = x.reshape(*SIZES, rows // size(DP), cols).transpose(*order, len(DP), len(DP) + 1)
    return x.reshape(size(NEAR), rows // size(NEAR), cols)


def local(acts, grad_out, proj_t, first_moment, second_moment):
    bf16 = jnp.bfloat16
    n_near, n_far, n_t = size(NEAR), size(FAR), 16
    rank = proj_t.shape[0]
    own = rank // (n_near * n_far)
    toks = acts.shape[0]
    inv_root = 1.0 / jnp.sqrt(jnp.float32(D))
    acts_all = to_all(acts, NEAR, n_near)
    grad_all = to_all(grad_out, NEAR, n_near)
    part = (dot(proj_t, acts, ((1,), (1,))) * inv_root).astype(bf16)
    mine = total(swap(part.reshape(n_t, rank // n_t, toks), TENSOR)).astype(bf16)
    coords = to_all(mine, TENSOR, n_t).reshape(rank, toks)
    coords = swap(by_near(coords), NEAR)
    grad_part = dot(coords, grad_all, ((0, 2), (0, 1))) / TOKENS
    per = rank // n_near
    grad_own = total(swap(grad_part.astype(bf16).reshape(n_far, own, -1), FAR))
    moment_one = 0.9 * first_moment + 0.1 * grad_own
    moment_two = 0.999 * second_moment + 0.001 * grad_own * grad_own
    adam_step = moment_one / (1.0 - 0.9**10) / (jnp.sqrt(moment_two / (1.0 - 0.999**10)) + 1e-08)
    low_own = grad_own.astype(bf16)
    low = to_all(low_own, FAR, n_far).reshape(per, -1)
    low_rows = to_all(low_own, NEAR, n_near).reshape(n_near * own, -1)
    grad_rows = jnp.concatenate([grad_all.reshape(n_near * toks, -1), low_rows], axis=0)
    both = dot(low, grad_rows, ((1,), (1,))).astype(bf16)
    pieces = both.reshape(n_t, per // n_t, -1)
    mine = total(swap(pieces, TENSOR)).astype(bf16)
    both = to_all(mine, TENSOR, n_t).reshape(per, -1)
    n_tok = n_near * toks
    pull = dot(both[:, :n_tok], acts_all.reshape(n_tok, -1), ((1,), (0,))) * (
        jnp.sqrt(jnp.float32(D)) / TOKENS
    )
    grid = proj_t.reshape(*SIZES, own, -1)
    for a in FAR:
        here = lax.axis_index(a)
        grid = lax.dynamic_slice_in_dim(grid, here, 1, DP.index(a))
    proj_rows = grid.reshape(n_near * own, -1)
    correction = dot(both[:, n_tok:], proj_rows, ((1,), (0,)))
    step = total(swap((pull - correction).astype(bf16).reshape(n_far, own, -1), FAR))
    place = lax.axis_index(DP) * own
    own_rows = lax.dynamic_slice_in_dim(proj_t, place, own, 0).astype(jnp.float32)
    return (adam_step, own_rows + step)


def solution(mesh):
    fine = Mesh(mesh.devices.reshape(*SIZES, 4, 4), DP + TENSOR)
    whole = P(DP, TENSOR)
    placed = (whole, whole, P(None, TENSOR), whole, whole)
    return jax.shard_map(
        local, mesh=fine, in_specs=placed, out_specs=(whole, whole), check_vma=False
    )
```

```python
import jax
import jax.numpy as jnp
from jax import lax
from jax.sharding import Mesh, PartitionSpec as P

D = 8192
TOKENS = 8192
DP = ("yh", "z", "c")
TENSOR = ("x", "yl")
OWN = 8


def swap(pieces, axes):
    return lax.all_to_all(pieces, axes, split_axis=0, concat_axis=0, tiled=True)


def to_all(x, axes, count):
    return swap(jnp.broadcast_to(x, (count, *x.shape)), axes)


def total(pieces):
    return jnp.sum(pieces.astype(jnp.float32), axis=0)


def dot(left, right, dims):
    return lax.dot_general(left, right, (dims, ((), ())), preferred_element_type=jnp.float32)


def pair(x, axis):
    return jnp.stack([x, lax.ppermute(x, axis, [(0, 1), (1, 0)])])


def near(x, axes):
    for axis in axes:
        x = pair(x, axis)
    return x


def from_own(x, axes):
    for dim, axis in enumerate(axes):
        x = jnp.where(lax.axis_index(axis) == 0, x, jnp.flip(x, dim))
    return x


def step(acts, grad_out, proj_t, first_moment, second_moment):
    bf16 = jnp.bfloat16
    root = jnp.sqrt(jnp.float32(D))
    grad_all = near(grad_out, ("yh", "c"))
    acts_all = near(acts, ("yh", "c"))
    rows = proj_t.reshape(2, 16, 2, OWN, -1)
    rows = lax.dynamic_index_in_dim(rows, lax.axis_index("z"), 1, keepdims=False)
    rows = from_own(rows, ("yh", "c")).reshape(4 * OWN, -1)
    own_rows = lax.dynamic_slice_in_dim(proj_t, lax.axis_index(DP) * OWN, OWN, 0)
    own_rows = lax.optimization_barrier(own_rows.astype(jnp.float32))
    part = (dot(proj_t, acts, ((1,), (1,))) * (1.0 / root)).astype(bf16)
    part = part.reshape(2, 4, 4, 2, OWN, 128).transpose(1, 3, 0, 2, 4, 5)
    got = swap(part.reshape(8, 64, 128), ("x", "c"))
    part = total(got.reshape(4, 2, 2, 4, OWN, 128)).astype(bf16)
    part = part.transpose(2, 1, 0, 3, 4)
    got = swap(part.reshape(8, 2 * OWN, 128), ("yl", "yh"))
    part = from_own(total(got.reshape(4, 2, 2, OWN, 128)), ("yh", "c")).astype(bf16)
    coords = to_all(part, TENSOR, 16)
    coords = coords.transpose(2, 1, 0, 3, 4).reshape(2, 2, 128, 128)
    grad_part = (dot(coords, grad_all, ((0, 1, 3), (0, 1, 2))) / TOKENS).astype(bf16)
    grad_own = total(swap(grad_part.reshape(16, OWN, -1), "z"))
    moment_one = 0.9 * first_moment + 0.1 * grad_own
    moment_two = 0.999 * second_moment + 0.001 * grad_own * grad_own
    adam_step = moment_one / (1.0 - 0.9**10) / (jnp.sqrt(moment_two / (1.0 - 0.999**10)) + 1e-08)
    low_own = grad_own.astype(bf16)
    low = to_all(low_own, "z", 16).reshape(128, -1)
    low_rows = near(low_own, ("c", "yh")).reshape(4 * OWN, -1)
    back = dot(low, grad_all.reshape(512, -1), ((1,), (1,))).astype(bf16)
    cross = dot(low, low_rows, ((1,), (1,))).astype(bf16)
    both = jnp.concatenate([back, cross], axis=1)
    both = total(swap(both.reshape(16, OWN, 544), TENSOR)).astype(bf16)
    both = to_all(both, TENSOR, 16).reshape(128, 544)
    pull = dot(both[:, :512], acts_all.reshape(512, -1), ((1,), (0,))) * (root / TOKENS)
    correction = dot(both[:, 512:], rows, ((1,), (0,)))
    moved = total(swap((pull - correction).astype(bf16).reshape(16, OWN, -1), "z"))
    return (adam_step, own_rows + moved)


def solution(mesh):
    fine = Mesh(mesh.devices.reshape(2, 16, 2, 4, 4), DP + TENSOR)
    whole = P(DP, TENSOR)
    placed = (whole, whole, P(None, TENSOR), whole, whole)
    return jax.shard_map(
        step, mesh=fine, in_specs=placed, out_specs=(whole, whole), check_vma=False
    )
```

```python
import jax
import jax.numpy as jnp
from jax import lax
from jax.sharding import Mesh, PartitionSpec as P

D = 8192
TOKENS = 8192
DP = ("yh", "z", "c")
TENSOR = ("x", "yl")
OWN = 8


def swap(pieces, axes):
    return lax.all_to_all(pieces, axes, split_axis=0, concat_axis=0, tiled=True)


def to_all(x, axes, count):
    return swap(jnp.broadcast_to(x, (count, *x.shape)), axes)


def total(pieces):
    return jnp.sum(pieces.astype(jnp.float32), axis=0)


def dot(left, right, dims):
    return lax.dot_general(left, right, (dims, ((), ())), preferred_element_type=jnp.float32)


def pair(x, axis):
    return jnp.stack([x, lax.ppermute(x, axis, [(0, 1), (1, 0)])])


def near(x, axes):
    for axis in axes:
        x = pair(x, axis)
    return x


def from_own(x, axes):
    for dim, axis in enumerate(axes):
        x = jnp.where(lax.axis_index(axis) == 0, x, jnp.flip(x, dim))
    return x


def step(acts, grad_out, proj_t, first_moment, second_moment):
    bf16 = jnp.bfloat16
    root = jnp.sqrt(jnp.float32(D))
    grad_all = near(grad_out, ("yh", "c"))
    acts_all = near(acts, ("yh", "c"))
    rows = proj_t.reshape(2, 16, 2, OWN, -1)
    rows = lax.dynamic_index_in_dim(rows, lax.axis_index("z"), 1, keepdims=False)
    rows = from_own(rows, ("yh", "c")).reshape(4 * OWN, -1)
    own_rows = lax.dynamic_slice_in_dim(proj_t, lax.axis_index(DP) * OWN, OWN, 0)
    own_rows = lax.optimization_barrier(own_rows.astype(jnp.float32))
    part = (dot(proj_t, acts, ((1,), (1,))) * (1.0 / root)).astype(bf16)
    got = swap(part.reshape(64, OWN, 128), ("yh", "x", "yl", "c"))
    part = jnp.sum(got.reshape(2, 16, 2, OWN, 128).astype(jnp.float32), axis=1)
    part = from_own(part, ("yh", "c")).astype(bf16)
    coords = to_all(part, TENSOR, 16)
    coords = coords.transpose(2, 1, 0, 3, 4).reshape(2, 2, 128, 128)
    grad_part = (dot(coords, grad_all, ((0, 1, 3), (0, 1, 2))) / TOKENS).astype(bf16)
    grad_own = total(swap(grad_part.reshape(16, OWN, -1), "z"))
    moment_one = 0.9 * first_moment + 0.1 * grad_own
    moment_two = 0.999 * second_moment + 0.001 * grad_own * grad_own
    adam_step = moment_one / (1.0 - 0.9**10) / (jnp.sqrt(moment_two / (1.0 - 0.999**10)) + 1e-08)
    low_own = grad_own.astype(bf16)
    low = to_all(low_own, "z", 16).reshape(128, -1)
    low_rows = near(low_own, ("c", "yh")).reshape(4 * OWN, -1)
    back = dot(low, grad_all.reshape(512, -1), ((1,), (1,))).astype(bf16)
    cross = dot(low, low_rows, ((1,), (1,))).astype(bf16)
    both = jnp.concatenate([back, cross], axis=1)
    both = total(swap(both.reshape(16, OWN, 544), TENSOR)).astype(bf16)
    both = to_all(both, TENSOR, 16).reshape(128, 544)
    pull = dot(both[:, :512], acts_all.reshape(512, -1), ((1,), (0,))) * (root / TOKENS)
    correction = dot(both[:, 512:], rows, ((1,), (0,)))
    moved = total(swap((pull - correction).astype(bf16).reshape(16, OWN, -1), "z"))
    return (adam_step, own_rows + moved)


def solution(mesh):
    fine = Mesh(mesh.devices.reshape(2, 16, 2, 4, 4), DP + TENSOR)
    whole = P(DP, TENSOR)
    placed = (whole, whole, P(None, TENSOR), whole, whole)
    return jax.shard_map(
        step, mesh=fine, in_specs=placed, out_specs=(whole, whole), check_vma=False
    )
```

```python
import jax
import jax.numpy as jnp
from jax import lax
from jax.sharding import Mesh, PartitionSpec as P

D = 8192
TOKENS = 8192
DP = ("yh", "z", "c")
TENSOR = ("x", "yl")
OWN = 8


def swap(pieces, axes):
    return lax.all_to_all(pieces, axes, split_axis=0, concat_axis=0, tiled=True)


def to_all(x, axes, count):
    return swap(jnp.broadcast_to(x, (count, *x.shape)), axes)


def total(pieces):
    return jnp.sum(pieces.astype(jnp.float32), axis=0)


def dot(left, right, dims):
    return lax.dot_general(left, right, (dims, ((), ())), preferred_element_type=jnp.float32)


def near(x, axes):
    for axis in axes:
        other = lax.ppermute(x, axis, [(0, 1), (1, 0)])
        x = lax.optimization_barrier(jnp.stack([x, other]))
    return x


def from_own(x, axes):
    for dim, axis in enumerate(axes):
        x = jnp.where(lax.axis_index(axis) == 0, x, jnp.flip(x, dim))
    return x


def step(acts, grad_out, proj_t, first_moment, second_moment):
    bf16 = jnp.bfloat16
    root = jnp.sqrt(jnp.float32(D))
    grad_all = near(grad_out, ("yh", "c"))
    acts_all = near(acts, ("c", "yh")).swapaxes(0, 1)
    rows = proj_t.reshape(2, 16, 2, OWN, -1)
    rows = lax.dynamic_index_in_dim(rows, lax.axis_index("z"), 1, keepdims=False)
    rows = from_own(rows, ("yh", "c")).reshape(4 * OWN, -1)
    own_rows = lax.dynamic_slice_in_dim(proj_t, lax.axis_index(DP) * OWN, OWN, 0)
    own_rows = lax.optimization_barrier(own_rows.astype(jnp.float32))
    part = (dot(proj_t, acts, ((1,), (1,))) * (1.0 / root)).astype(bf16)
    got = swap(part.reshape(64, OWN, 128), ("yh", "x", "yl", "c"))
    part = jnp.sum(got.reshape(2, 16, 2, OWN, 128).astype(jnp.float32), axis=1)
    part = from_own(part, ("yh", "c")).astype(bf16)
    coords = to_all(part, TENSOR, 16)
    coords = coords.transpose(2, 1, 0, 3, 4).reshape(2, 2, 128, 128)
    grad_part = (dot(coords, grad_all, ((0, 1, 3), (0, 1, 2))) / TOKENS).astype(bf16)
    grad_own = total(swap(grad_part.reshape(16, OWN, -1), "z"))
    low_own = grad_own.astype(bf16)
    low_own, grad_own = lax.optimization_barrier((low_own, grad_own))
    moment_one = 0.9 * first_moment + 0.1 * grad_own
    moment_two = 0.999 * second_moment + 0.001 * grad_own * grad_own
    root_two = jnp.sqrt(moment_two / (1.0 - 0.999**10)) + 1e-08
    adam_step = moment_one / (1.0 - 0.9**10) / root_two
    low = to_all(low_own, "z", 16).reshape(128, -1)
    low_rows = near(low_own, ("c", "yh")).reshape(4 * OWN, -1)
    back = dot(low, grad_all.reshape(512, -1), ((1,), (1,))).astype(bf16)
    cross = dot(low, low_rows, ((1,), (1,))).astype(bf16)
    both = jnp.concatenate([back, cross], axis=1)
    both = total(swap(both.reshape(16, OWN, 544), TENSOR)).astype(bf16)
    both = to_all(both, TENSOR, 16).reshape(128, 544)
    pull = dot(both[:, :512], acts_all.reshape(512, -1), ((1,), (0,))) * (root / TOKENS)
    correction = dot(both[:, 512:], rows, ((1,), (0,)))
    moved = total(swap((pull - correction).astype(bf16).reshape(16, OWN, -1), "z"))
    return (adam_step, own_rows + moved)


def solution(mesh):
    fine = Mesh(mesh.devices.reshape(2, 16, 2, 4, 4), DP + TENSOR)
    whole = P(DP, TENSOR)
    placed = (whole, whole, P(None, TENSOR), whole, whole)
    return jax.shard_map(
        step, mesh=fine, in_specs=placed, out_specs=(whole, whole), check_vma=False
    )
```

```python
import jax
import jax.numpy as jnp
from jax import lax
from jax.sharding import Mesh, PartitionSpec as P

D = 8192
TOKENS = 8192
DP = ("yh", "z", "c")
TENSOR = ("x", "yl")
OWN = 8


def swap(pieces, axes):
    return lax.all_to_all(pieces, axes, split_axis=0, concat_axis=0, tiled=True)


def to_all(x, axes, count):
    return swap(jnp.broadcast_to(x, (count, *x.shape)), axes)


def total(pieces):
    return jnp.sum(pieces.astype(jnp.float32), axis=0)


def dot(left, right, dims):
    return lax.dot_general(left, right, (dims, ((), ())), preferred_element_type=jnp.float32)


def near(x, axes):
    for axis in axes:
        other = lax.ppermute(x, axis, [(0, 1), (1, 0)])
        x = lax.optimization_barrier(jnp.stack([x, other]))
    return x


def from_own(x, axes):
    for dim, axis in enumerate(axes):
        x = jnp.where(lax.axis_index(axis) == 0, x, jnp.flip(x, dim))
    return x


def step(acts, grad_out, proj_t, first_moment, second_moment):
    bf16 = jnp.bfloat16
    root = jnp.sqrt(jnp.float32(D))
    grad_all = near(grad_out, ("yh", "c"))
    acts_here = near(acts, ("c",))
    acts_there = lax.ppermute(acts_here, "yh", [(0, 1), (1, 0)])
    rows = proj_t.reshape(2, 16, 2, OWN, -1)
    rows = lax.dynamic_index_in_dim(rows, lax.axis_index("z"), 1, keepdims=False)
    rows = from_own(rows, ("yh", "c")).reshape(4 * OWN, -1)
    own_rows = lax.dynamic_slice_in_dim(proj_t, lax.axis_index(DP) * OWN, OWN, 0)
    own_rows = own_rows.astype(jnp.float32)
    part = (dot(proj_t, acts, ((1,), (1,))) * (1.0 / root)).astype(bf16)
    got = swap(part.reshape(64, OWN, 128), ("yh", "x", "yl", "c"))
    part = jnp.sum(got.reshape(2, 16, 2, OWN, 128).astype(jnp.float32), axis=1)
    part = from_own(part, ("yh", "c")).astype(bf16)
    coords = to_all(part, TENSOR, 16)
    coords = coords.transpose(2, 1, 0, 3, 4).reshape(2, 2, 128, 128)
    grad_part = (dot(coords, grad_all, ((0, 1, 3), (0, 1, 2))) / TOKENS).astype(bf16)
    grad_own = total(swap(grad_part.reshape(16, OWN, -1), "z"))
    low_own = grad_own.astype(bf16)
    low_own, grad_own = lax.optimization_barrier((low_own, grad_own))
    moment_one = 0.9 * first_moment + 0.1 * grad_own
    moment_two = 0.999 * second_moment + 0.001 * grad_own * grad_own
    root_two = jnp.sqrt(moment_two / (1.0 - 0.999**10)) + 1e-08
    adam_step = moment_one / (1.0 - 0.9**10) / root_two
    low = to_all(low_own, "z", 16).reshape(128, -1)
    low_rows = near(low_own, ("c", "yh")).reshape(4 * OWN, -1)
    low, low_rows, own_rows, adam_step = lax.optimization_barrier(
        (low, low_rows, own_rows, adam_step)
    )
    back = dot(low, grad_all.reshape(512, -1), ((1,), (1,))).astype(bf16)
    cross = dot(low, low_rows, ((1,), (1,))).astype(bf16)
    both = jnp.concatenate([back, cross], axis=1)
    both = total(swap(both.reshape(16, OWN, 544), TENSOR)).astype(bf16)
    both = to_all(both, TENSOR, 16).reshape(128, 544)
    back = both[:, :512].reshape(128, 2, 2, 128)
    pull = dot(back[:, :, 0], acts_here, ((1, 2), (0, 1)))
    pull = (pull + dot(back[:, :, 1], acts_there, ((1, 2), (0, 1)))) * (root / TOKENS)
    correction = dot(both[:, 512:], rows, ((1,), (0,)))
    moved = total(swap((pull - correction).astype(bf16).reshape(16, OWN, -1), "z"))
    return (adam_step, own_rows + moved)


def solution(mesh):
    fine = Mesh(mesh.devices.reshape(2, 16, 2, 4, 4), DP + TENSOR)
    whole = P(DP, TENSOR)
    placed = (whole, whole, P(None, TENSOR), whole, whole)
    return jax.shard_map(
        step, mesh=fine, in_specs=placed, out_specs=(whole, whole), check_vma=False
    )
```

```python
import jax
import jax.numpy as jnp
from jax import lax
from jax.sharding import Mesh, PartitionSpec as P

D = 8192
TOKENS = 8192
DP = ("yh", "z", "c")
TENSOR = ("x", "yl")
OWN = 8


def swap(pieces, axes):
    return lax.all_to_all(pieces, axes, split_axis=0, concat_axis=0, tiled=True)


def to_all(x, axes, count):
    return swap(jnp.broadcast_to(x, (count, *x.shape)), axes)


def total(pieces):
    return jnp.sum(pieces.astype(jnp.float32), axis=0)


def dot(left, right, dims):
    return lax.dot_general(left, right, (dims, ((), ())), preferred_element_type=jnp.float32)


def across(x, axis):
    return lax.ppermute(x, axis, [(0, 1), (1, 0)])


def near(x, axes):
    for axis in axes:
        other = across(x, axis)
        x = lax.optimization_barrier(jnp.stack([x, other]))
    return x


def from_own(x, axes):
    for dim, axis in enumerate(axes):
        x = jnp.where(lax.axis_index(axis) == 0, x, jnp.flip(x, dim))
    return x


def step(acts, grad_out, proj_t, first_moment, second_moment):
    bf16 = jnp.bfloat16
    root = jnp.sqrt(jnp.float32(D))
    grad_yh = across(grad_out, "yh")
    grad_c = across(grad_out, "c")
    grad_d = across(grad_yh, "c")
    grad_all = jnp.stack([grad_out, grad_yh, grad_c, grad_d]).reshape(2, 2, 128, -1)
    acts_here = near(acts, ("c",))
    acts_there = across(acts_here, "yh")
    rows = proj_t.reshape(2, 16, 2, OWN, -1)
    rows = lax.dynamic_index_in_dim(rows, lax.axis_index("z"), 1, keepdims=False)
    rows = from_own(rows, ("yh", "c")).reshape(4 * OWN, -1)
    own_rows = lax.dynamic_slice_in_dim(proj_t, lax.axis_index(DP) * OWN, OWN, 0)
    own_rows = own_rows.astype(jnp.float32)
    part = (dot(proj_t, acts, ((1,), (1,))) * (1.0 / root)).astype(bf16)
    got = swap(part.reshape(64, OWN, 128), ("yh", "x", "yl", "c"))
    got, own_rows = lax.optimization_barrier((got, own_rows))
    part = jnp.sum(got.reshape(2, 16, 2, OWN, 128).astype(jnp.float32), axis=1)
    part = from_own(part, ("yh", "c")).astype(bf16)
    coords = to_all(part, TENSOR, 16)
    coords = coords.transpose(2, 1, 0, 3, 4).reshape(2, 2, 128, 128)
    grad_part = (dot(coords, grad_all, ((0, 1, 3), (0, 1, 2))) / TOKENS).astype(bf16)
    got = swap(grad_part.reshape(16, OWN, -1), "z")
    got, rows = lax.optimization_barrier((got, rows))
    grad_own = total(got)
    low_own = grad_own.astype(bf16)
    low_own, grad_own = lax.optimization_barrier((low_own, grad_own))
    moment_one = 0.9 * first_moment + 0.1 * grad_own
    moment_two = 0.999 * second_moment + 0.001 * grad_own * grad_own
    root_two = jnp.sqrt(moment_two / (1.0 - 0.999**10)) + 1e-08
    adam_step = moment_one / (1.0 - 0.9**10) / root_two
    low = to_all(low_own, "z", 16).reshape(128, -1)
    low_rows = near(low_own, ("c", "yh")).reshape(4 * OWN, -1)
    low, low_rows, adam_step = lax.optimization_barrier((low, low_rows, adam_step))
    back = dot(low, grad_all.reshape(512, -1), ((1,), (1,))).astype(bf16)
    cross = dot(low, low_rows, ((1,), (1,))).astype(bf16)
    both = jnp.concatenate([back, cross], axis=1)
    both = total(swap(both.reshape(16, OWN, 544), TENSOR)).astype(bf16)
    both = to_all(both, TENSOR, 16).reshape(128, 544)
    back = both[:, :512].reshape(128, 2, 2, 128)
    pull = dot(back[:, :, 0], acts_here, ((1, 2), (0, 1)))
    pull = (pull + dot(back[:, :, 1], acts_there, ((1, 2), (0, 1)))) * (root / TOKENS)
    correction = dot(both[:, 512:], rows, ((1,), (0,)))
    moved = total(swap((pull - correction).astype(bf16).reshape(16, OWN, -1), "z"))
    return (adam_step, own_rows + moved)


def solution(mesh):
    fine = Mesh(mesh.devices.reshape(2, 16, 2, 4, 4), DP + TENSOR)
    whole = P(DP, TENSOR)
    placed = (whole, whole, P(None, TENSOR), whole, whole)
    return jax.shard_map(
        step, mesh=fine, in_specs=placed, out_specs=(whole, whole), check_vma=False
    )
```

```python
import jax
import jax.numpy as jnp
from jax import lax
from jax.sharding import Mesh, PartitionSpec as P

D = 8192
TOKENS = 8192
DP = ("yh", "z", "c")
TENSOR = ("x", "yl")
OWN = 8


def swap(pieces, axes):
    return lax.all_to_all(pieces, axes, split_axis=0, concat_axis=0, tiled=True)


def to_all(x, axes, count):
    return swap(jnp.broadcast_to(x, (count, *x.shape)), axes)


def total(pieces):
    return jnp.sum(pieces.astype(jnp.float32), axis=0)


def dot(left, right, dims):
    return lax.dot_general(left, right, (dims, ((), ())), preferred_element_type=jnp.float32)


def across(x, *axes):
    last = 2 ** len(axes) - 1
    return lax.ppermute(x, axes, [(i, last - i) for i in range(last + 1)])


def from_own(x, axes):
    for dim, axis in enumerate(axes):
        x = jnp.where(lax.axis_index(axis) == 0, x, jnp.flip(x, dim))
    return x


def step(acts, grad_out, proj_t, first_moment, second_moment):
    bf16 = jnp.bfloat16
    root = jnp.sqrt(jnp.float32(D))
    grad_yh = across(grad_out, "yh")
    grad_c = across(grad_out, "c")
    grad_d = across(grad_yh, "c")
    grad_all = jnp.stack([grad_out, grad_c, grad_yh, grad_d]).reshape(2, 2, 128, -1)
    acts_c = across(acts, "c")
    acts_here = lax.optimization_barrier(jnp.concatenate([acts, acts_c]))
    acts_there = across(acts_here, "yh")
    rows = proj_t.reshape(2, 16, 2, OWN, -1)
    rows = lax.dynamic_index_in_dim(rows, lax.axis_index("z"), 1, keepdims=False)
    rows = from_own(rows, ("yh", "c")).reshape(4 * OWN, -1)
    own_rows = lax.dynamic_slice_in_dim(proj_t, lax.axis_index(DP) * OWN, OWN, 0)
    own_rows = own_rows.astype(jnp.float32)
    part = (dot(proj_t, acts, ((1,), (1,))) * (1.0 / root)).astype(bf16)
    got = swap(part.reshape(64, OWN, 128), ("yh", "x", "yl", "c"))
    got, own_rows = lax.optimization_barrier((got, own_rows))
    part = jnp.sum(got.reshape(2, 16, 2, OWN, 128).astype(jnp.float32), axis=1)
    part = from_own(part, ("yh", "c")).astype(bf16)
    coords = to_all(part, TENSOR, 16)
    coords = coords.transpose(1, 2, 0, 3, 4).reshape(2, 2, 128, 128)
    grad_part = (dot(coords, grad_all, ((0, 1, 3), (0, 1, 2))) / TOKENS).astype(bf16)
    got = swap(grad_part.reshape(16, OWN, -1), "z")
    got, rows = lax.optimization_barrier((got, rows))
    grad_own = total(got)
    low_own = grad_own.astype(bf16)
    low_own, grad_own = lax.optimization_barrier((low_own, grad_own))
    moment_one = 0.9 * first_moment + 0.1 * grad_own
    moment_two = 0.999 * second_moment + 0.001 * grad_own * grad_own
    root_two = jnp.sqrt(moment_two / (1.0 - 0.999**10)) + 1e-08
    adam_step = moment_one / (1.0 - 0.9**10) / root_two
    low = to_all(low_own, "z", 16).reshape(128, -1)
    low_yh = across(low_own, "yh")
    low_d = across(low_own, "yh", "c")
    low_c = across(low_own, "c")
    low_rows = jnp.concatenate([low_own, low_c, low_yh, low_d])
    low, low_rows, adam_step = lax.optimization_barrier((low, low_rows, adam_step))
    back = dot(low, grad_all.reshape(512, -1), ((1,), (1,))).astype(bf16)
    cross = dot(low, low_rows, ((1,), (1,))).astype(bf16)
    both = jnp.concatenate([back, cross], axis=1)
    both = total(swap(both.reshape(16, OWN, 544), TENSOR)).astype(bf16)
    both = to_all(both, TENSOR, 16).reshape(128, 544)
    pull = dot(both[:, :256], acts_here, ((1,), (0,)))
    pull = (pull + dot(both[:, 256:512], acts_there, ((1,), (0,)))) * (root / TOKENS)
    correction = dot(both[:, 512:], rows, ((1,), (0,)))
    moved = total(swap((pull - correction).astype(bf16).reshape(16, OWN, -1), "z"))
    return (adam_step, own_rows + moved)


def solution(mesh):
    fine = Mesh(mesh.devices.reshape(2, 16, 2, 4, 4), DP + TENSOR)
    whole = P(DP, TENSOR)
    placed = (whole, whole, P(None, TENSOR), whole, whole)
    return jax.shard_map(
        step, mesh=fine, in_specs=placed, out_specs=(whole, whole), check_vma=False
    )
```

```python
import jax
import jax.numpy as jnp
from jax import lax
from jax.sharding import Mesh, PartitionSpec as P

D = 8192
TOKENS = 8192
DP = ("yh", "z", "c")
TENSOR = ("x", "yl")
OWN = 8


def swap(pieces, axes):
    return lax.all_to_all(pieces, axes, split_axis=0, concat_axis=0, tiled=True)


def to_all(x, axes, count):
    return swap(jnp.broadcast_to(x, (count, *x.shape)), axes)


def total(pieces):
    return jnp.sum(pieces.astype(jnp.float32), axis=0)


def dot(left, right, dims):
    return lax.dot_general(left, right, (dims, ((), ())), preferred_element_type=jnp.float32)


def across(x, *axes):
    last = 2 ** len(axes) - 1
    return lax.ppermute(x, axes, [(i, last - i) for i in range(last + 1)])


def from_own(x, axes):
    for dim, axis in enumerate(axes):
        x = jnp.where(lax.axis_index(axis) == 0, x, jnp.flip(x, dim))
    return x


def step(acts, grad_out, proj_t, first_moment, second_moment):
    bf16 = jnp.bfloat16
    root = jnp.sqrt(jnp.float32(D))
    grad_yh = across(grad_out, "yh")
    grad_c = across(grad_out, "c")
    grad_d = across(grad_yh, "c")
    grad_all = jnp.stack([grad_out, grad_c, grad_yh, grad_d]).reshape(2, 2, 128, -1)
    moment_base = 0.9 * first_moment
    own_rows = lax.dynamic_slice_in_dim(proj_t, lax.axis_index(DP) * OWN, OWN, 0)
    own_rows = own_rows.astype(jnp.float32)
    part = (dot(proj_t, acts, ((1,), (1,))) * (1.0 / root)).astype(bf16)
    got = swap(part.reshape(64, OWN, 128), ("yh", "x", "yl", "c"))
    got, moment_base = lax.optimization_barrier((got, moment_base))
    part = jnp.sum(got.reshape(2, 16, 2, OWN, 128).astype(jnp.float32), axis=1)
    part = from_own(part, ("yh", "c")).astype(bf16)
    coords = to_all(part, TENSOR, 16).transpose(1, 2, 0, 3, 4)
    grad_part = (dot(coords, grad_all, ((0, 1, 4), (0, 1, 2))) / TOKENS).astype(bf16)
    got = swap(grad_part.reshape(16, OWN, -1), "z")
    coords_yh = across(coords[1, 0], "yh")
    coords_d = across(coords[1, 1], "yh", "c")
    coords_c = across(coords[0, 1], "c")
    mine = jnp.stack([coords[0, 0], coords_c, coords_yh, coords_d])
    mine = from_own(mine.reshape(2, 2, 16, OWN, 128), ("yh", "c"))
    mine = mine.transpose(0, 2, 1, 3, 4).reshape(512, 128)
    residual = (root * acts - dot(mine, proj_t, ((0,), (0,)))).astype(bf16)
    residual_yh = across(residual, "yh")
    residual_c = across(residual, "c")
    residual_d = across(residual_yh, "c")
    residual_all = jnp.concatenate([residual, residual_c, residual_yh, residual_d])
    got, own_rows = lax.optimization_barrier((got, own_rows))
    grad_own = total(got)
    low_own = grad_own.astype(bf16)
    low_own, grad_own = lax.optimization_barrier((low_own, grad_own))
    moment_one = moment_base + 0.1 * grad_own
    moment_two = 0.999 * second_moment + 0.001 * grad_own * grad_own
    root_two = jnp.sqrt(moment_two / (1.0 - 0.999**10)) + 1e-08
    adam_step = moment_one / (1.0 - 0.9**10) / root_two
    low = to_all(low_own, "z", 16).reshape(128, -1)
    low, residual_all, adam_step = lax.optimization_barrier((low, residual_all, adam_step))
    back = dot(low, grad_all.reshape(512, -1), ((1,), (1,))).astype(bf16)
    back = total(swap(back.reshape(16, OWN, -1), TENSOR)).astype(bf16)
    back = to_all(back, TENSOR, 16).reshape(128, -1)
    pull = (dot(back, residual_all, ((1,), (0,))) / TOKENS).astype(bf16)
    moved = total(swap(pull.reshape(16, OWN, -1), "z"))
    return (adam_step, own_rows + moved)


def solution(mesh):
    fine = Mesh(mesh.devices.reshape(2, 16, 2, 4, 4), DP + TENSOR)
    whole = P(DP, TENSOR)
    placed = (whole, whole, P(None, TENSOR), whole, whole)
    return jax.shard_map(
        step, mesh=fine, in_specs=placed, out_specs=(whole, whole), check_vma=False
    )
```

```python
import jax
import jax.numpy as jnp
from jax import lax
from jax.sharding import Mesh, PartitionSpec as P

D = 8192
TOKENS = 8192
DP = ("yh", "z", "c")
TENSOR = ("x", "yl")
OWN = 8


def swap(pieces, axes):
    return lax.all_to_all(pieces, axes, split_axis=0, concat_axis=0, tiled=True)


def to_all(x, axes, count):
    return swap(jnp.broadcast_to(x, (count, *x.shape)), axes)


def total(pieces):
    return jnp.sum(pieces.astype(jnp.float32), axis=0)


def dot(left, right, dims):
    return lax.dot_general(left, right, (dims, ((), ())), preferred_element_type=jnp.float32)


def across(x, *axes):
    last = 2 ** len(axes) - 1
    return lax.ppermute(x, axes, [(i, last - i) for i in range(last + 1)])


def from_own(x, axes):
    for dim, axis in enumerate(axes):
        x = jnp.where(lax.axis_index(axis) == 0, x, jnp.flip(x, dim))
    return x


def step(acts, grad_out, proj_t, first_moment, second_moment):
    bf16 = jnp.bfloat16
    root = jnp.sqrt(jnp.float32(D))
    grad_yh = across(grad_out, "yh")
    grad_c = across(grad_out, "c")
    grad_d = across(grad_yh, "c")
    grad_all = jnp.stack([grad_out, grad_c, grad_yh, grad_d]).reshape(2, 2, 128, -1)
    moment_base = 0.9 * first_moment
    own_rows = lax.dynamic_slice_in_dim(proj_t, lax.axis_index(DP) * OWN, OWN, 0)
    own_rows = own_rows.astype(jnp.float32)
    part = (dot(proj_t, acts, ((1,), (1,))) * (1.0 / root)).astype(bf16)
    got = swap(part.reshape(64, OWN, 128), ("yh", "x", "yl", "c"))
    got, moment_base = lax.optimization_barrier((got, moment_base))
    part = jnp.sum(got.reshape(2, 16, 2, OWN, 128).astype(jnp.float32), axis=1)
    part = from_own(part, ("yh", "c")).astype(bf16)
    coords = to_all(part, TENSOR, 16).transpose(1, 2, 0, 3, 4)
    grad_part = (dot(coords, grad_all, ((0, 1, 4), (0, 1, 2))) / TOKENS).astype(bf16)
    got = swap(grad_part.reshape(16, OWN, -1), "z")
    coords_yh = across(coords[1, 0], "yh")
    coords_d = across(coords[1, 1], "yh", "c")
    coords_c = across(coords[0, 1], "c")
    mine = jnp.stack([coords[0, 0], coords_c, coords_yh, coords_d])
    mine = from_own(mine.reshape(2, 2, 16, OWN, 128), ("yh", "c"))
    mine = mine.transpose(0, 2, 1, 3, 4).reshape(512, 128)
    residual = (root * acts - dot(mine, proj_t, ((0,), (0,)))).astype(bf16)
    residual_yh = across(residual, "yh")
    residual_c = across(residual, "c")
    residual_d = across(residual, "yh", "c")
    residual_here = jnp.concatenate([residual, residual_c])
    grad_own = total(got)
    low_own = grad_own.astype(bf16)
    low_own, grad_own = lax.optimization_barrier((low_own, grad_own))
    moment_one = moment_base + 0.1 * grad_own
    moment_two = 0.999 * second_moment + 0.001 * grad_own * grad_own
    root_two = jnp.sqrt(moment_two / (1.0 - 0.999**10)) + 1e-08
    adam_step = moment_one / (1.0 - 0.9**10) / root_two
    low = to_all(low_own, "z", 16).reshape(128, -1)
    low, residual_here, own_rows, adam_step = lax.optimization_barrier(
        (low, residual_here, own_rows, adam_step)
    )
    back = dot(low, grad_all.reshape(512, -1), ((1,), (1,))).astype(bf16)
    back = total(swap(back.reshape(16, OWN, -1), TENSOR)).astype(bf16)
    back = to_all(back, TENSOR, 16).reshape(128, -1)
    pull = dot(back[:, 256:384], residual_yh, ((1,), (0,)))
    pull = pull + dot(back[:, 384:], residual_d, ((1,), (0,)))
    pull = (pull + dot(back[:, :256], residual_here, ((1,), (0,)))) / TOKENS
    moved = total(swap(pull.astype(bf16).reshape(16, OWN, -1), "z"))
    return (adam_step, own_rows + moved)


def solution(mesh):
    fine = Mesh(mesh.devices.reshape(2, 16, 2, 4, 4), DP + TENSOR)
    whole = P(DP, TENSOR)
    placed = (whole, whole, P(None, TENSOR), whole, whole)
    return jax.shard_map(
        step, mesh=fine, in_specs=placed, out_specs=(whole, whole), check_vma=False
    )
```

```python
import jax
import jax.numpy as jnp
from jax import lax
from jax.sharding import Mesh, PartitionSpec as P

D = 8192
TOKENS = 8192
DP = ("yh", "z", "c")
TENSOR = ("x", "yl")
OWN = 8


def swap(pieces, axes):
    return lax.all_to_all(pieces, axes, split_axis=0, concat_axis=0, tiled=True)


def to_all(x, axes, count):
    return swap(jnp.broadcast_to(x, (count, *x.shape)), axes)


def total(pieces):
    return jnp.sum(pieces.astype(jnp.float32), axis=0)


def dot(left, right, dims):
    return lax.dot_general(left, right, (dims, ((), ())), preferred_element_type=jnp.float32)


def across(x, *axes):
    last = 2 ** len(axes) - 1
    return lax.ppermute(x, axes, [(i, last - i) for i in range(last + 1)])


def from_own(x, axes):
    for dim, axis in enumerate(axes):
        x = jnp.where(lax.axis_index(axis) == 0, x, jnp.flip(x, dim))
    return x


def step(acts, grad_out, proj_t, first_moment, second_moment):
    bf16 = jnp.bfloat16
    root = jnp.sqrt(jnp.float32(D))
    grad_yh = across(grad_out, "yh")
    grad_c = across(grad_out, "c")
    grad_d = across(grad_yh, "c")
    grad_all = jnp.stack([grad_out, grad_c, grad_yh, grad_d]).reshape(2, 2, 128, -1)
    acts_c = across(acts, "c")
    acts_yh = across(acts, "yh")
    acts_d = across(acts_yh, "c")
    moment_base = 0.9 * first_moment
    own_rows = lax.dynamic_slice_in_dim(proj_t, lax.axis_index(DP) * OWN, OWN, 0)
    own_rows = own_rows.astype(jnp.float32)
    part = (dot(proj_t, acts, ((1,), (1,))) * (1.0 / root)).astype(bf16)
    got = swap(part.reshape(64, OWN, 128), ("yh", "x", "yl", "c"))
    got, moment_base = lax.optimization_barrier((got, moment_base))
    part = jnp.sum(got.reshape(2, 16, 2, OWN, 128).astype(jnp.float32), axis=1)
    part = from_own(part, ("yh", "c")).astype(bf16)
    coords = to_all(part, TENSOR, 16)
    grad_part = (dot(coords, grad_all, ((1, 2, 4), (0, 1, 2))) / TOKENS).astype(bf16)
    got = swap(grad_part.reshape(16, OWN, -1), "z")
    got, own_rows = lax.optimization_barrier((got, own_rows))
    coords_yh = across(coords, "yh")
    coords_d = across(coords, "yh", "c")
    coords_c = across(coords, "c")
    ranks = [coords, jnp.flip(coords_c, 2), jnp.flip(coords_yh, 1), jnp.flip(coords_d, (1, 2))]
    ranks = from_own(jnp.stack(ranks).reshape(2, 2, *coords.shape), ("yh", "c"))
    acts_all = jnp.concatenate([acts, acts_c, acts_yh, acts_d])
    ranks = ranks.transpose(0, 2, 1, 5, 3, 4, 6).reshape(512, 512)
    spanned = dot(ranks, proj_t, ((0,), (0,)))
    residual = (root * acts_all - spanned).astype(bf16)
    grad_own = total(got)
    low_own = grad_own.astype(bf16)
    low_own, grad_own = lax.optimization_barrier((low_own, grad_own))
    moment_one = moment_base + 0.1 * grad_own
    moment_two = 0.999 * second_moment + 0.001 * grad_own * grad_own
    root_two = jnp.sqrt(moment_two / (1.0 - 0.999**10)) + 1e-08
    adam_step = moment_one / (1.0 - 0.9**10) / root_two
    low = to_all(low_own, "z", 16).reshape(128, -1)
    low, residual, adam_step = lax.optimization_barrier((low, residual, adam_step))
    back = dot(low, grad_all.reshape(512, -1), ((1,), (1,))).astype(bf16)
    back = total(swap(back.reshape(16, OWN, -1), TENSOR)).astype(bf16)
    back = to_all(back, TENSOR, 16).reshape(128, -1)
    pull = dot(back, residual, ((1,), (0,))) / TOKENS
    moved = total(swap(pull.astype(bf16).reshape(16, OWN, -1), "z"))
    return (adam_step, own_rows + moved)


def solution(mesh):
    fine = Mesh(mesh.devices.reshape(2, 16, 2, 4, 4), DP + TENSOR)
    whole = P(DP, TENSOR)
    placed = (whole, whole, P(None, TENSOR), whole, whole)
    return jax.shard_map(
        step, mesh=fine, in_specs=placed, out_specs=(whole, whole), check_vma=False
    )
```
